32 devices in a mesh: facet: 8 (over y, x, core), sub: 4 (over z).
Axes of the slice: x: 2, y: 2, z: 4, core: 2. Of those that a mesh axis runs over, the one named last changes fastest.
Arguments:
- facet_model: bfloat16 [8, 512, 8192], P('facet', 'sub'), may hold values from -6 to 6
- column_offsets: int32 [8], replicated, may hold values from 0 to 65024
- row_offsets: int32 [2], replicated, may hold values from 0 to 65024
- block_column: int32 [8, 4, 32], P('facet', 'sub'), may hold values from 0 to 1
- cell_rows: int32 [8, 4, 4096], P('facet', 'sub'), may hold values from 0 to 127
- cell_columns: int32 [8, 4, 4096], P('facet', 'sub'), may hold values from 0 to 508
- cell_fraction: float32 [8, 4, 2, 4096], P('facet', 'sub'), may hold values from 0 to 1
Outputs:
- visibilities: float32 [8, 4, 2, 4096], P('facet', 'sub')
The draws below stay inside these ranges and needn't reach their ends.
Inputs may be any that keep to these rules, and one draw needn't show every extreme that they name: `block_column`: each aligned block of 128 visibilities lies in one of the 2 subgrid columns of its group.
All inputs are finite; a program needn't handle non-finite values.
Results may differ from the reference program's by a relative error of at most 0.0043.
Values may be sent and summed in bfloat16 or wider, within the bound.
A program may use at most 128 MiB of HBM per device.

```python
import math
import jax
import jax.numpy as jnp
from jax import lax

FX = 8192
GRID = 65536
FACETS = 8
FR = 512
SW = 512
SCD = 2
SR = 2
VIS_DEV = 4096
U = 1024
SV = 1024
SC = 8
SVD = 128
NBLK = 32
N_FACET = 8
N_SUB = 4


def plant(array, key, smallest, high):
    shape = array.shape
    index_at = [jax.random.randint(jax.random.fold_in(key, axis), (), 0, shape[axis]) for axis in range(len(shape))]
    array = array.at[tuple(index_at)].set(smallest)
    longest = shape.index(max(shape))
    index_at[longest] = (index_at[longest] + 1) % shape[longest]
    return array.at[tuple(index_at)].set(high)


def shard_levels(key, shape, pieces, least, largest):
    level, own = 1.0, jax.random.fold_in(key, 6)
    for axis_at, shards_of in pieces:
        draws = jnp.exp(jax.random.uniform(jax.random.fold_in(own, axis_at), (shards_of,), jnp.float32, least / len(pieces), largest / len(pieces)))
        level = level * jnp.repeat(draws, shape[axis_at] // shards_of).reshape([-1 if axis == axis_at else 1 for axis in range(len(shape))])
    return level


def scatter_about(own_key, extent, scale, reach, pieces=(), kind=jnp.bfloat16):
    array = scale * jax.random.normal(own_key, extent, jnp.float32)
    if pieces:
        array = array * shard_levels(own_key, extent, pieces, -0.22, 0.18)
    return jnp.clip(array, -reach, reach).astype(kind)


def setup_inputs(seed: int = 0) -> dict:
    arg_keys = jax.random.split(jax.random.key(seed), 8)
    return {
        "facet_model": scatter_about(arg_keys[0], (FACETS, FR, FX), 1.0, 6.0, ((0, 8), (1, 4))),
        "column_offsets": plant(jax.random.randint(arg_keys[1], (SC,), 0, GRID - SW + 1), jax.random.fold_in(arg_keys[1], 1), 0, GRID - SW).astype(jnp.int32),
        "row_offsets": jax.random.randint(arg_keys[2], (SR,), 0, GRID - SW + 1).astype(jnp.int32),
        "block_column": plant(jax.random.randint(arg_keys[3], (N_FACET, N_SUB, NBLK), 0, SCD), jax.random.fold_in(arg_keys[3], 1), 0, SCD - 1).astype(jnp.int32),
        "cell_rows": plant(jax.random.randint(arg_keys[4], (N_FACET, N_SUB, VIS_DEV), 0, SVD), jax.random.fold_in(arg_keys[4], 1), 0, SVD - 1).astype(jnp.int32),
        "cell_columns": plant(jax.random.randint(arg_keys[5], (N_FACET, N_SUB, VIS_DEV), 0, SW - 3), jax.random.fold_in(arg_keys[5], 1), 0, (SW - 3) - 1).astype(jnp.int32),
        "cell_fraction": jnp.clip(1.0 * jax.random.uniform(arg_keys[6], (N_FACET, N_SUB, 2, VIS_DEV), jnp.float32) ** shard_levels(arg_keys[6], (N_FACET, N_SUB, 2, VIS_DEV), ((0, 8), (1, 4)), -0.2, 0.2), 0.0, 1.0),
    }


two_pi = 2.0 * math.pi
spread = 0.98

def angles(outer_index, inner_index, grid_size):
    high_part = inner_index // 256
    low_part = inner_index % 256
    upper_turns = outer_index[:, None] * high_part[None, :] % grid_size
    whole_turns = (upper_turns * 256 + outer_index[:, None] * low_part[None, :]) % grid_size
    return whole_turns.astype(jnp.float32) * (two_pi / grid_size)

def first_table(x_positions, u_positions, grid_size):
    phase_angle = angles(x_positions, u_positions, grid_size)
    return jnp.concatenate([jnp.cos(phase_angle), -jnp.sin(phase_angle)], axis=1).astype(jnp.bfloat16)

def second_term(spectra, v_positions, y_positions, half_width, grid_size):
    phase_angle = angles(v_positions, y_positions, grid_size)
    cosine = jnp.cos(phase_angle).astype(jnp.bfloat16)
    sine_part = jnp.sin(phase_angle).astype(jnp.bfloat16)
    first_product = jnp.dot(cosine, spectra, preferred_element_type=jnp.float32)
    second_product = jnp.dot(sine_part, spectra, preferred_element_type=jnp.float32)
    real_part = first_product[:, :half_width] + second_product[:, half_width:]
    imaginary = first_product[:, half_width:] - second_product[:, :half_width]
    return jnp.concatenate([real_part, imaginary], axis=1)

def kernel_taps(fraction):
    offsets = jnp.arange(4).astype(fraction.dtype)
    distance = offsets[:, None] - 1.0 - fraction[None, :]
    return jnp.exp(-distance * distance / spread)

def degrid(spectrum, cell_rows, cell_column, fraction, half_width, scale_factor):
    flat_real = spectrum[:, :half_width].reshape(-1)
    flat_imag = spectrum[:, half_width:].reshape(-1)
    row_taps = kernel_taps(fraction[0])
    column_taps = kernel_taps(fraction[1])
    total_real = jnp.zeros(cell_rows.shape, spectrum.dtype)
    total_imag = jnp.zeros(cell_rows.shape, spectrum.dtype)
    for shift_row in range(4):
        for shift_column in range(4):
            flat_index = (cell_rows + shift_row) * half_width + cell_column + shift_column
            weight = row_taps[shift_row] * column_taps[shift_column]
            total_real = total_real + weight * jnp.take(flat_real, flat_index)
            total_imag = total_imag + weight * jnp.take(flat_imag, flat_index)
    return jnp.stack([total_real, total_imag]) * scale_factor

def reference(facet_model, column_offsets, row_offsets, block_column, cell_rows, cell_columns, cell_fraction):
    strip = SV // N_FACET
    scale_factor = 1.0 / math.sqrt(FACETS * FR * FX)
    u_stride = GRID // FX
    v_stride = GRID // SW
    v_positions = (row_offsets[:, None] + v_stride * jnp.arange(SW, dtype=jnp.int32)[None, :]).reshape(-1)
    facet_ids = jnp.arange(FACETS, dtype=jnp.int32)

    def one_group(sub_group):
        starts = lax.dynamic_slice_in_dim(column_offsets, (sub_group * SCD).astype(jnp.int32), SCD)
        u_positions = (starts[:, None] + u_stride * jnp.arange(SW, dtype=jnp.int32)[None, :]).reshape(-1)

        def add_facet(total, item):
            facet_rows, facet_id = item
            x_positions = facet_id % 8 * FX + jnp.arange(FX, dtype=jnp.int32)
            y_positions = facet_id // 8 * FX + jnp.arange(FR, dtype=jnp.int32)
            spectra = jnp.dot(facet_rows, first_table(x_positions, u_positions, GRID), preferred_element_type=jnp.float32).astype(jnp.bfloat16)
            return (total + second_term(spectra, v_positions, y_positions, U, GRID), None)
        spectrum, unused = lax.scan(add_facet, jnp.zeros((SV, 2 * U), jnp.float32), (facet_model, facet_ids))
        padded = jnp.concatenate([spectrum, jnp.zeros((3, 2 * U), jnp.float32)], axis=0)
        rows_all = (jnp.arange(N_FACET, dtype=jnp.int32)[:, None] * strip + cell_rows[:, sub_group, :]).reshape(-1)
        columns = jnp.repeat(block_column[:, sub_group, :], 128, axis=1) * SW + cell_columns[:, sub_group, :]
        fraction = jnp.moveaxis(cell_fraction[:, sub_group], 1, 0).reshape(2, -1)
        result = degrid(padded, rows_all, columns.reshape(-1), fraction, U, scale_factor)
        return result.reshape(2, N_FACET, VIS_DEV)
    stacked = lax.map(one_group, jnp.arange(N_SUB, dtype=jnp.int32))
    return jnp.transpose(stacked, (2, 0, 1, 3))
```

```python
import functools
import math

import jax
import jax.numpy as jnp
from jax import lax
from jax.experimental import pallas as pl
from jax.experimental.pallas import tpu as pltpu
from jax.sharding import PartitionSpec as P

MESH = pl.DeviceIdType.MESH
FX = 8192
GRID = 65536
FR = 512
SW = 512
SCD = 2
ROW_FACETS = 8
HALO = 16
CHUNK = 128
DEPTH = 512
SPREAD = 0.98


def cos_sin(turns):
    quadrant = (turns + GRID // 8) >> 14
    rest = turns - (quadrant << 14)
    theta = rest.astype(jnp.float32) * (2.0 * math.pi / GRID)
    t2 = theta * theta
    sine = theta * (1.0 + t2 * (-1.0 / 6 + t2 * (1.0 / 120 + t2 * (-1.0 / 5040 + t2 * (1.0 / 362880)))))
    cosine = 1.0 + t2 * (-0.5 + t2 * (1.0 / 24 + t2 * (-1.0 / 720 + t2 * (1.0 / 40320 - t2 * (1.0 / 3628800)))))
    odd = (quadrant & 1) == 1
    c = jnp.where(odd, sine, cosine)
    s = jnp.where(odd, cosine, sine)
    c = jnp.where(((quadrant + 1) & 2) == 2, -c, c)
    s = jnp.where((quadrant & 2) == 2, -s, s)
    return c, s


def predict_kernel(
    nf, ns, rows, strip, scale,
    columns_hbm, rows_hbm, block_hbm, x_hbm, cell_v_hbm, cell_u_hbm, fraction_hbm, out_ref,
    columns_ref, rows_ref, block_ref, cell_v_ref, cell_u_ref, fraction_ref, x_ref, table0, table1, turn0, turn1, pair0, pair1, sib_send, sib_recv,
    send1, recv1, send2, recv2, vy, send3, recv3, weights, planes,
    in_sems, ssem0, rsem0, ssem1, rsem1, ssem2, rsem2, ssem3, rsem3,
):
    bf16, f32 = jnp.bfloat16, jnp.float32
    facet = lax.axis_index("facet")
    sub = lax.axis_index("sub")
    frow = facet // ROW_FACETS
    fcol = facet % ROW_FACETS
    base = frow * ROW_FACETS
    chip = fcol // 2
    core = fcol % 2
    parts = FX // DEPTH
    chips = ROW_FACETS // 2
    steps = chips * ns
    high = strip + HALO

    loads = [
        pltpu.make_async_copy(source, target, in_sems.at[n])
        for n, (source, target) in enumerate([
            (columns_hbm, columns_ref), (rows_hbm, rows_ref), (x_hbm, x_ref), (block_hbm, block_ref),
            (cell_v_hbm, cell_v_ref), (cell_u_hbm, cell_u_ref), (fraction_hbm, fraction_ref),
        ])
    ]
    for load in loads:
        load.start()
    barrier = pltpu.get_barrier_semaphore()
    for k in range(1, nf):
        pl.semaphore_signal(barrier, inc=1, device_id={"facet": (facet + k) % nf}, device_id_type=MESH)
    for k in range(1, ns):
        pl.semaphore_signal(barrier, inc=1, device_id={"sub": (sub + k) % ns}, device_id_type=MESH)

    def place(t):
        far = chips - 1 - t % chips
        other = (chip // 2 + far // 2) % 2 * 2 + (chip % 2 + far % 2) % 2
        return other, (sub + 1 + t // chips) % ns

    x_first = fcol * FX

    def step_turns(t, turn):
        q, group = place(t)
        lane = lax.broadcasted_iota(jnp.int32, (64, 256), 1)
        line = lax.broadcasted_iota(jnp.int32, (64, 256), 0)
        u = columns_ref[group * SCD + q // 2] + 8 * (q % 2 * 256 + lane)
        x = jnp.where(line < 32, 16 * line, jnp.where(line < 48, line - 32, x_first + DEPTH * (line - 48)))
        c, s = cos_sin((x * u) & (GRID - 1))
        turn[0] = c
        turn[1] = s

    def table_rows(turn, table, first, last):
        fc, fs = turn[0, 32:48], turn[1, 32:48]
        for g in range(first, last):
            c0, s0 = turn[0, g:g + 1], turn[1, g:g + 1]
            table[g * 16:(g + 1) * 16, 0:256] = (c0 * fc - s0 * fs).astype(bf16)
            table[g * 16:(g + 1) * 16, 256:512] = (s0 * fc + c0 * fs).astype(bf16)

    def build_vy():
        y = frow * FX + lax.broadcasted_iota(jnp.int32, (16, FR), 1)
        low = lax.broadcasted_iota(jnp.int32, (16, FR), 0)
        fine_c, fine_s = cos_sin((128 * low * y) & (GRID - 1))
        for r in range(2):
            yh = frow * FX + lax.broadcasted_iota(jnp.int32, (32, FR), 1)
            upper = rows_ref[r] + 2048 * lax.broadcasted_iota(jnp.int32, (32, FR), 0)
            cc, cs = cos_sin((upper * yh) & (GRID - 1))
            for g in range(32):
                at = r * SW + g * 16
                c0, s0 = cc[g:g + 1], cs[g:g + 1]
                vy[0, at:at + 16, :] = (c0 * fine_c - s0 * fine_s).astype(bf16)
                vy[1, at:at + 16, :] = (s0 * fine_c + c0 * fine_s).astype(bf16)
        vy[:, 2 * SW:, :] = jnp.zeros((2, HALO, FR), bf16)

    def copy0(t):
        return pltpu.make_async_remote_copy(
            src_ref=sib_send.at[t], dst_ref=sib_recv.at[t],
            send_sem=ssem0.at[t], recv_sem=rsem0.at[t],
            device_id={"facet": base + 2 * chip + 1 - core}, device_id_type=MESH,
        )

    def copy1(target, group, source):
        return pltpu.make_async_remote_copy(
            src_ref=send1.at[target, group], dst_ref=recv1.at[source, group],
            send_sem=ssem1.at[target, group], recv_sem=rsem1.at[source, group],
            device_id={"facet": base + 2 * target + core}, device_id_type=MESH,
        )

    def copy2(target, source):
        return pltpu.make_async_remote_copy(
            src_ref=send2.at[target], dst_ref=recv2.at[source],
            send_sem=ssem2.at[target], recv_sem=rsem2.at[source],
            device_id={"sub": target}, device_id_type=MESH,
        )

    def copy3(target, source):
        return pltpu.make_async_remote_copy(
            src_ref=send3.at[target], dst_ref=recv3.at[source],
            send_sem=ssem3.at[target], recv_sem=rsem3.at[source],
            device_id={"facet": target}, device_id_type=MESH,
        )

    def compute(t, table, turn, pair, next_table, next_turn, gate=None):
        step_turns((t + 1) % steps, next_turn)
        group_rows = min(rows, 16)
        count = rows // group_rows
        for r in range(count):
            at = r * group_rows
            left = jnp.concatenate([x_ref[at + h:at + h + 16, a * DEPTH:(a + 1) * DEPTH] for h in range(0, group_rows, 16) for a in range(parts)], axis=0)
            z = jnp.dot(left, table[...], preferred_element_type=f32)
            for h in range(0, group_rows, 16):
                real = jnp.zeros((16, 256), f32)
                imag = jnp.zeros((16, 256), f32)
                for a in range(parts):
                    zc = z[h * parts + a * 16:h * parts + (a + 1) * 16, 0:256]
                    zs = z[h * parts + a * 16:h * parts + (a + 1) * 16, 256:512]
                    wc, ws = turn[0, 48 + a:49 + a], turn[1, 48 + a:49 + a]
                    real = real + (wc * zc - ws * zs)
                    imag = imag - (ws * zc + wc * zs)
                for k in range(2):
                    pair[k, at + h:at + h + 16, 0:128] = real[:, k * 128:(k + 1) * 128]
                    pair[k, at + h:at + h + 16, 128:256] = imag[:, k * 128:(k + 1) * 128]
            table_rows(next_turn, next_table, r * 32 // count, (r + 1) * 32 // count)
        sib_send[t] = pair[1 - core].astype(bf16)
        if gate is not None:
            @pl.when(gate)
            def _():
                pl.semaphore_wait(barrier, nf - 1 + ns - 1)
        copy0(t).start()

    def combine(t, pair):
        q, group = place(t)
        copy0(t).wait_recv()
        send1[q, group] = (pair[core] + sib_recv[t].astype(f32)).astype(bf16)

        @pl.when(t % chips != chips - 1)
        def _():
            copy1(q, group, chip).start()

    def gather(group):
        for j in range(1, chips):
            copy1(chip, group, (chip + j) % chips).wait_recv()
        total = send1[chip, group].astype(f32)
        for j in range(1, chips):
            total = total + recv1[(chip + j) % chips, group].astype(f32)
        return total.astype(bf16)

    loads[0].wait()
    loads[1].wait()
    step_turns(0, turn0)
    table_rows(turn0, table0, 0, 32)
    build_vy()
    loads[2].wait()

    def two_steps(m, carry):
        t = 2 * m
        compute(t, table0, turn0, pair0, table1, turn1, m == 0)

        @pl.when(m > 0)
        def _():
            combine(t - 1, pair1)

        @pl.when((m % 2 == 1) & (m > 2))
        def _():
            group = (sub + m // 2) % ns
            send2[group] = gather(group)
            copy2(group, sub).start()

        compute(t + 1, table1, turn1, pair1, table0, turn0)
        combine(t, pair0)
        return carry

    lax.fori_loop(0, steps // 2, two_steps, 0)
    combine(steps - 1, pair1)
    recv2[sub] = gather(sub)
    for k in range(1, ns):
        copy2(sub, (sub + k) % ns).wait_recv()

    partial = recv2[...].reshape(ns * rows, 2 * CHUNK)

    for k in range(1, nf + 1):
        target = (facet + k) % nf
        at = pl.ds(pl.multiple_of(target * strip, 16), high)
        first = jnp.dot(vy[0, at, :], partial, preferred_element_type=f32)
        second = jnp.dot(vy[1, at, :], partial, preferred_element_type=f32)
        send3[target, :, 0:128] = (first[:, 0:128] + second[:, 128:256]).astype(bf16)
        send3[target, :, 128:256] = (first[:, 128:256] - second[:, 0:128]).astype(bf16)
        if k < nf:
            copy3(target, facet).start()

    recv3[facet] = send3[facet]

    for load in loads[3:]:
        load.wait()
    blocks = cell_v_ref.shape[1] // 128
    root = math.sqrt(math.log2(math.e) / SPREAD)

    def taps(cell, fraction, extent):
        position = lax.broadcasted_iota(jnp.int32, (extent, 128), 0)
        offset = position.astype(f32) * root - (cell.astype(f32) + 1.0 + fraction) * root
        distance = position - cell
        return jnp.where((distance & -4) == 0, jnp.exp2(-(offset * offset)), 0.0)

    def build_weights(b, carry):
        at = pl.ds(pl.multiple_of(b * 128, 128), 128)
        w = taps(cell_u_ref[:, at], fraction_ref[1:2, at], SW)
        upper = w.astype(bf16)
        weights[b, :, 0:128] = upper
        weights[b, :, 128:256] = (w - upper.astype(f32)).astype(bf16)
        return carry

    lax.fori_loop(0, blocks, build_weights, 0, unroll=2)

    def drain0(t, carry):
        copy0(t).wait_send()
        return carry

    def drain1(n, carry):
        copy1((chip + 1 + n // ns) % chips, n % ns, chip).wait_send()
        return carry

    lax.fori_loop(0, steps, drain0, 0)
    lax.fori_loop(0, (chips - 1) * ns, drain1, 0)
    for k in range(1, ns):
        copy2((sub + k) % ns, sub).wait_send()
    for k in range(1, nf):
        copy3(facet, (facet + k) % nf).wait_recv()
    for column in range(SCD):
        for j in range(SW // CHUNK):
            chunk = column * (SW // CHUNK) + j
            total = recv3[chunk]
            if nf > ROW_FACETS:
                total = total.astype(f32)
                for other in range(1, nf // ROW_FACETS):
                    total = total + recv3[other * ROW_FACETS + chunk].astype(f32)
                total = total.astype(bf16)
            planes[column, 0:high, j * 128:(j + 1) * 128] = total[:, 0:128]
            planes[column, high:2 * high, j * 128:(j + 1) * 128] = total[:, 128:256]

    def degrid(b, carry):
        at = pl.ds(pl.multiple_of(b * 128, 128), 128)
        mixed = jnp.dot(planes[block_ref[b]], weights[b], preferred_element_type=f32)
        mixed = mixed[:, 0:128] + mixed[:, 128:256]
        row_weight = taps(cell_v_ref[:, at], fraction_ref[0:1, at], high) * scale
        out_ref[0:1, at] = jnp.sum(mixed[:high] * row_weight, axis=0, keepdims=True)
        out_ref[1:2, at] = jnp.sum(mixed[high:] * row_weight, axis=0, keepdims=True)
        return carry

    lax.fori_loop(0, blocks, degrid, 0, unroll=16)

    for k in range(1, nf):
        copy3((facet + k) % nf, facet).wait_send()


def per_device(
    facet_model, column_offsets, row_offsets, block_column, cell_rows, cell_columns, cell_fraction
):
    nf = lax.axis_size("facet")
    ns = lax.axis_size("sub")
    rows = facet_model.shape[1]
    strip = 2 * SW // nf
    high = strip + HALO
    total = cell_rows.shape[-1]
    blocks = total // 128
    chips = ROW_FACETS // 2
    steps = chips * ns
    vmem = pl.BlockSpec(memory_space=pltpu.VMEM)
    bf16, f32 = jnp.bfloat16, jnp.float32
    sems = pltpu.SemaphoreType.DMA
    result = pl.pallas_call(
        functools.partial(predict_kernel, nf, ns, rows, strip, 1.0 / math.sqrt(nf * FR * FX)),
        out_shape=jax.ShapeDtypeStruct((2, total), f32),
        in_specs=[pl.BlockSpec(memory_space=pltpu.HBM)] * 7,
        out_specs=vmem,
        scratch_shapes=[
            pltpu.SMEM(column_offsets.shape, jnp.int32),
            pltpu.SMEM(row_offsets.shape, jnp.int32),
            pltpu.SMEM((blocks,), jnp.int32),
            pltpu.VMEM((1, total), jnp.int32),
            pltpu.VMEM((1, total), jnp.int32),
            pltpu.VMEM((2, total), f32),
            pltpu.VMEM((rows, FX), bf16),
            pltpu.VMEM((DEPTH, 512), bf16),
            pltpu.VMEM((DEPTH, 512), bf16),
            pltpu.VMEM((2, 64, 256), f32),
            pltpu.VMEM((2, 64, 256), f32),
            pltpu.VMEM((2, rows, 256), f32),
            pltpu.VMEM((2, rows, 256), f32),
            pltpu.VMEM((steps, rows, 256), bf16),
            pltpu.VMEM((steps, rows, 256), bf16),
            pltpu.VMEM((chips, ns, rows, 256), bf16),
            pltpu.VMEM((chips, ns, rows, 256), bf16),
            pltpu.VMEM((ns, rows, 256), bf16),
            pltpu.VMEM((ns, rows, 256), bf16),
            pltpu.VMEM((2, 2 * SW + HALO, FR), bf16),
            pltpu.VMEM((nf, high, 256), bf16),
            pltpu.VMEM((nf, high, 256), bf16),
            pltpu.VMEM((blocks, SW, 256), bf16),
            pltpu.VMEM((SCD, 2 * high, SW), bf16),
            sems((7,)),
            sems((steps,)), sems((steps,)),
            sems((chips, ns)), sems((chips, ns)),
            sems((ns,)), sems((ns,)),
            sems((nf,)), sems((nf,)),
        ],
        compiler_params=pltpu.CompilerParams(
            collective_id=0, has_side_effects=True, vmem_limit_bytes=56 * 1024 * 1024
        ),
    )(
        column_offsets, row_offsets, block_column[0, 0], facet_model[0],
        cell_rows[0], cell_columns[0], cell_fraction[0, 0],
    )
    return result[None, None]


def solution(mesh):
    in_specs = (
        P("facet", "sub", None),
        P(),
        P(),
        P("facet", "sub", None),
        P("facet", "sub", None),
        P("facet", "sub", None),
        P("facet", "sub", None, None),
    )
    out_specs = P("facet", "sub", None, None)
    return jax.shard_map(
        per_device, mesh=mesh, in_specs=in_specs, out_specs=out_specs, check_vma=False
    )
```

```python
import functools
import math

import jax
import jax.numpy as jnp
from jax import lax
from jax.experimental import pallas as pl
from jax.experimental.pallas import tpu as pltpu
from jax.sharding import PartitionSpec as P

MESH = pl.DeviceIdType.MESH
FX = 8192
GRID = 65536
FR = 512
SW = 512
SCD = 2
ROW_FACETS = 8
HALO = 16
CHUNK = 128
DEPTH = 1024
HALF = DEPTH // 2
GROUP = 32
SPREAD = 0.98


def cos_sin(turns, whole=GRID):
    shift = (whole // 4).bit_length() - 1
    quadrant = (turns + whole // 8) >> shift
    rest = turns - (quadrant << shift)
    theta = rest.astype(jnp.float32) * (2.0 * math.pi / whole)
    t2 = theta * theta
    sine = theta * (1.0 + t2 * (-1.0 / 6 + t2 * (1.0 / 120 + t2 * (-1.0 / 5040 + t2 * (1.0 / 362880)))))
    cosine = 1.0 + t2 * (-0.5 + t2 * (1.0 / 24 + t2 * (-1.0 / 720 + t2 * (1.0 / 40320 - t2 * (1.0 / 3628800)))))
    odd = (quadrant & 1) == 1
    c = jnp.where(odd, sine, cosine)
    s = jnp.where(odd, cosine, sine)
    c = jnp.where(((quadrant + 1) & 2) == 2, -c, c)
    s = jnp.where((quadrant & 2) == 2, -s, s)
    return c, s


def predict_kernel(
    nf, ns, rows, strip, scale,
    columns_hbm, rows_hbm, block_hbm, x_hbm, cell_v_hbm, cell_u_hbm, fraction_hbm, out_ref,
    columns_ref, rows_ref, block_ref, cell_v_ref, cell_u_ref, fraction_ref, x_ref, even_ref, odd_ref, table0, table1, turn0, turn1, pair0, pair1, sib_send, sib_recv,
    send1, recv1, own, send2, recv2, vy, send3, recv3, weights, planes,
    in_sems, ssem0, rsem0, ssem1, rsem1, ssem2, rsem2, ssem3, rsem3,
):
    bf16, f32 = jnp.bfloat16, jnp.float32
    facet = lax.axis_index("facet")
    sub = lax.axis_index("sub")
    frow = facet // ROW_FACETS
    fcol = facet % ROW_FACETS
    base = frow * ROW_FACETS
    chip = fcol // 2
    core = fcol % 2
    parts = FX // DEPTH
    chips = ROW_FACETS // 2
    steps = chips * ns
    high = strip + HALO

    loads = [
        pltpu.make_async_copy(source, target, in_sems.at[n])
        for n, (source, target) in enumerate([
            (columns_hbm, columns_ref), (rows_hbm, rows_ref), (x_hbm, x_ref), (block_hbm, block_ref),
            (cell_v_hbm, cell_v_ref), (cell_u_hbm, cell_u_ref), (fraction_hbm, fraction_ref),
        ])
    ]
    for load in loads:
        load.start()
    barrier = pltpu.get_barrier_semaphore()
    for k in range(1, nf):
        pl.semaphore_signal(barrier, inc=1, device_id={"facet": (facet + k) % nf}, device_id_type=MESH)
    for k in range(1, ns):
        pl.semaphore_signal(barrier, inc=1, device_id={"sub": (sub + k) % ns}, device_id_type=MESH)

    def place(t):
        far = chips - 1 - t % chips
        other = (chip // 2 + far // 2) % 2 * 2 + (chip % 2 + far % 2) % 2
        return other, (sub + 1 + t // chips) % ns

    x_first = fcol * FX

    def step_turns(t, turn):
        q, group = place(t)
        lane = lax.broadcasted_iota(jnp.int32, (64, 256), 1)
        line = lax.broadcasted_iota(jnp.int32, (64, 256), 0)
        u = columns_ref[group * SCD + q // 2] + 8 * (q % 2 * 256 + lane)
        x = jnp.where(line < 32, 32 * line, jnp.where(line < 48, 2 * (line - 32) + 1, 2 * (x_first + DEPTH * (line - 48)) + DEPTH - 1))
        c, s = cos_sin((x * u) & (2 * GRID - 1), 2 * GRID)
        turn[0] = c
        turn[1] = s

    def table_rows(turn, table, first, last):
        fc, fs = turn[0, 32:48], turn[1, 32:48]
        for g in range(first, last):
            c0, s0 = turn[0, g:g + 1], turn[1, g:g + 1]
            table[g * 16:(g + 1) * 16, 0:256] = (c0 * fc - s0 * fs).astype(bf16)
            table[g * 16:(g + 1) * 16, 256:512] = (s0 * fc + c0 * fs).astype(bf16)

    def fold():
        line = lax.broadcasted_iota(jnp.int32, (256, 256), 0)
        lane = lax.broadcasted_iota(jnp.int32, (256, 256), 1)
        flip = jnp.where(line + lane == 255, 1.0, 0.0).astype(bf16)
        for a in range(parts):
            for k in range(HALF // 256):
                low = x_ref[:, a * DEPTH + HALF - (k + 1) * 256:a * DEPTH + HALF - k * 256]
                low = jnp.dot(low, flip, preferred_element_type=f32)
                high_half = x_ref[:, a * DEPTH + HALF + k * 256:a * DEPTH + HALF + (k + 1) * 256].astype(f32)
                even = (high_half + low).astype(bf16)
                odd = (high_half - low).astype(bf16)
                for r in range(rows // 16):
                    at = (r * parts + a) * 16
                    even_ref[at:at + 16, k * 256:(k + 1) * 256] = even[r * 16:(r + 1) * 16]
                    odd_ref[at:at + 16, k * 256:(k + 1) * 256] = odd[r * 16:(r + 1) * 16]

    def build_vy():
        y = frow * FX + lax.broadcasted_iota(jnp.int32, (16, FR), 1)
        low = lax.broadcasted_iota(jnp.int32, (16, FR), 0)
        fine_c, fine_s = cos_sin((128 * low * y) & (GRID - 1))
        for r in range(2):
            yh = frow * FX + lax.broadcasted_iota(jnp.int32, (32, FR), 1)
            upper = rows_ref[r] + 2048 * lax.broadcasted_iota(jnp.int32, (32, FR), 0)
            cc, cs = cos_sin((upper * yh) & (GRID - 1))
            for g in range(32):
                at = r * SW + g * 16
                c0, s0 = cc[g:g + 1], cs[g:g + 1]
                vy[0, at:at + 16, :] = (c0 * fine_c - s0 * fine_s).astype(bf16)
                vy[1, at:at + 16, :] = (s0 * fine_c + c0 * fine_s).astype(bf16)
        vy[:, 2 * SW:, :] = jnp.zeros((2, HALO, FR), bf16)

    def copy0(t):
        return pltpu.make_async_remote_copy(
            src_ref=sib_send.at[t], dst_ref=sib_recv.at[t],
            send_sem=ssem0.at[t], recv_sem=rsem0.at[t],
            device_id={"facet": base + 2 * chip + 1 - core}, device_id_type=MESH,
        )

    def copy1(target, group, source):
        return pltpu.make_async_remote_copy(
            src_ref=send1.at[target, group], dst_ref=recv1.at[source, group],
            send_sem=ssem1.at[target, group], recv_sem=rsem1.at[source, group],
            device_id={"facet": base + 2 * target + core}, device_id_type=MESH,
        )

    def copy2(target, source):
        return pltpu.make_async_remote_copy(
            src_ref=send2.at[target], dst_ref=recv2.at[source],
            send_sem=ssem2.at[target], recv_sem=rsem2.at[source],
            device_id={"sub": target}, device_id_type=MESH,
        )

    def copy3(target, source):
        return pltpu.make_async_remote_copy(
            src_ref=send3.at[target], dst_ref=recv3.at[source],
            send_sem=ssem3.at[target], recv_sem=rsem3.at[source],
            device_id={"facet": target}, device_id_type=MESH,
        )

    def compute(t, table, turn, pair, next_table, next_turn, gate=None):
        step_turns((t + 1) % steps, next_turn)
        group_rows = min(rows, GROUP)
        count = rows // group_rows
        for r in range(count):
            at = r * group_rows
            lines = pl.ds(at * parts, group_rows * parts)
            zc_all = jnp.dot(even_ref[lines, :], table[:, 0:256], preferred_element_type=f32)
            zs_all = jnp.dot(odd_ref[lines, :], table[:, 256:512], preferred_element_type=f32)
            for h in range(0, group_rows, 16):
                real = jnp.zeros((16, 256), f32)
                imag = jnp.zeros((16, 256), f32)
                for a in range(parts):
                    zc = zc_all[h * parts + a * 16:h * parts + (a + 1) * 16]
                    zs = zs_all[h * parts + a * 16:h * parts + (a + 1) * 16]
                    wc, ws = turn[0, 48 + a:49 + a], turn[1, 48 + a:49 + a]
                    real = real + (wc * zc - ws * zs)
                    imag = imag - (ws * zc + wc * zs)
                for k in range(2):
                    pair[k, at + h:at + h + 16, 0:128] = real[:, k * 128:(k + 1) * 128]
                    pair[k, at + h:at + h + 16, 128:256] = imag[:, k * 128:(k + 1) * 128]
            table_rows(next_turn, next_table, r * 32 // count, (r + 1) * 32 // count)
        sib_send[t] = pair[1 - core]
        if gate is not None:
            @pl.when(gate)
            def _():
                pl.semaphore_wait(barrier, nf - 1 + ns - 1)
        copy0(t).start()

    def combine(t, pair):
        q, group = place(t)
        copy0(t).wait_recv()
        both = pair[core] + sib_recv[t]

        @pl.when(t % chips != chips - 1)
        def _():
            send1[q, group] = both.astype(bf16)
            copy1(q, group, chip).start()

        @pl.when(t % chips == chips - 1)
        def _():
            own[group] = both

    def gather(group):
        for j in range(1, chips):
            copy1(chip, group, (chip + j) % chips).wait_recv()
        total = own[group]
        for j in range(1, chips):
            total = total + recv1[(chip + j) % chips, group].astype(f32)
        return total.astype(bf16)

    loads[0].wait()
    loads[1].wait()
    step_turns(0, turn0)
    table_rows(turn0, table0, 0, 32)
    build_vy()
    loads[2].wait()
    fold()

    def two_steps(m, carry):
        t = 2 * m
        compute(t, table0, turn0, pair0, table1, turn1, m == 0)

        @pl.when(m > 0)
        def _():
            combine(t - 1, pair1)

        @pl.when((m % 2 == 1) & (m > 2))
        def _():
            group = (sub + m // 2) % ns
            send2[group] = gather(group)
            copy2(group, sub).start()

        compute(t + 1, table1, turn1, pair1, table0, turn0)
        combine(t, pair0)
        return carry

    lax.fori_loop(0, steps // 2, two_steps, 0)
    combine(steps - 1, pair1)
    recv2[sub] = gather(sub)
    for k in range(1, ns):
        copy2(sub, (sub + k) % ns).wait_recv()

    partial = recv2[...].reshape(ns * rows, 2 * CHUNK)

    for k in range(1, nf + 1):
        target = (facet + k) % nf
        at = pl.ds(pl.multiple_of(target * strip, 16), high)
        first = jnp.dot(vy[0, at, :], partial, preferred_element_type=f32)
        second = jnp.dot(vy[1, at, :], partial, preferred_element_type=f32)
        send3[target, :, 0:128] = (first[:, 0:128] + second[:, 128:256]).astype(bf16)
        send3[target, :, 128:256] = (first[:, 128:256] - second[:, 0:128]).astype(bf16)
        if k < nf:
            copy3(target, facet).start()

    recv3[facet] = send3[facet]

    for load in loads[3:]:
        load.wait()
    blocks = cell_v_ref.shape[1] // 128
    root = math.sqrt(math.log2(math.e) / SPREAD)

    def taps(cell, fraction, extent):
        position = lax.broadcasted_iota(jnp.int32, (extent, 128), 0)
        offset = position.astype(f32) * root - (cell.astype(f32) + 1.0 + fraction) * root
        distance = position - cell
        return jnp.where((distance & -4) == 0, jnp.exp2(-(offset * offset)), 0.0)

    def build_weights(b, carry):
        at = pl.ds(pl.multiple_of(b * 128, 128), 128)
        w = taps(cell_u_ref[:, at], fraction_ref[1:2, at], SW)
        upper = w.astype(bf16)
        weights[b, :, 0:128] = upper
        weights[b, :, 128:256] = (w - upper.astype(f32)).astype(bf16)
        return carry

    lax.fori_loop(0, blocks, build_weights, 0, unroll=2)

    def drain0(t, carry):
        copy0(t).wait_send()
        return carry

    def drain1(n, carry):
        copy1((chip + 1 + n // ns) % chips, n % ns, chip).wait_send()
        return carry

    lax.fori_loop(0, steps, drain0, 0)
    lax.fori_loop(0, (chips - 1) * ns, drain1, 0)
    for k in range(1, ns):
        copy2((sub + k) % ns, sub).wait_send()
    for k in range(1, nf):
        copy3(facet, (facet + k) % nf).wait_recv()
    for column in range(SCD):
        for j in range(SW // CHUNK):
            chunk = column * (SW // CHUNK) + j
            total = recv3[chunk]
            if nf > ROW_FACETS:
                total = total.astype(f32)
                for other in range(1, nf // ROW_FACETS):
                    total = total + recv3[other * ROW_FACETS + chunk].astype(f32)
                total = total.astype(bf16)
            planes[column, 0:high, j * 128:(j + 1) * 128] = total[:, 0:128]
            planes[column, high:2 * high, j * 128:(j + 1) * 128] = total[:, 128:256]

    def degrid(b, carry):
        at = pl.ds(pl.multiple_of(b * 128, 128), 128)
        mixed = jnp.dot(planes[block_ref[b]], weights[b], preferred_element_type=f32)
        mixed = mixed[:, 0:128] + mixed[:, 128:256]
        row_weight = taps(cell_v_ref[:, at], fraction_ref[0:1, at], high) * scale
        out_ref[0:1, at] = jnp.sum(mixed[:high] * row_weight, axis=0, keepdims=True)
        out_ref[1:2, at] = jnp.sum(mixed[high:] * row_weight, axis=0, keepdims=True)
        return carry

    lax.fori_loop(0, blocks, degrid, 0, unroll=16)

    for k in range(1, nf):
        copy3((facet + k) % nf, facet).wait_send()


def per_device(
    facet_model, column_offsets, row_offsets, block_column, cell_rows, cell_columns, cell_fraction
):
    nf = lax.axis_size("facet")
    ns = lax.axis_size("sub")
    rows = facet_model.shape[1]
    strip = 2 * SW // nf
    high = strip + HALO
    total = cell_rows.shape[-1]
    blocks = total // 128
    chips = ROW_FACETS // 2
    steps = chips * ns
    vmem = pl.BlockSpec(memory_space=pltpu.VMEM)
    bf16, f32 = jnp.bfloat16, jnp.float32
    sems = pltpu.SemaphoreType.DMA
    result = pl.pallas_call(
        functools.partial(predict_kernel, nf, ns, rows, strip, 1.0 / math.sqrt(nf * FR * FX)),
        out_shape=jax.ShapeDtypeStruct((2, total), f32),
        in_specs=[pl.BlockSpec(memory_space=pltpu.HBM)] * 7,
        out_specs=vmem,
        scratch_shapes=[
            pltpu.SMEM(column_offsets.shape, jnp.int32),
            pltpu.SMEM(row_offsets.shape, jnp.int32),
            pltpu.SMEM((blocks,), jnp.int32),
            pltpu.VMEM((1, total), jnp.int32),
            pltpu.VMEM((1, total), jnp.int32),
            pltpu.VMEM((2, total), f32),
            pltpu.VMEM((rows, FX), bf16),
            pltpu.VMEM((rows * FX // DEPTH, HALF), bf16),
            pltpu.VMEM((rows * FX // DEPTH, HALF), bf16),
            pltpu.VMEM((HALF, 512), bf16),
            pltpu.VMEM((HALF, 512), bf16),
            pltpu.VMEM((2, 64, 256), f32),
            pltpu.VMEM((2, 64, 256), f32),
            pltpu.VMEM((2, rows, 256), f32),
            pltpu.VMEM((2, rows, 256), f32),
            pltpu.VMEM((steps, rows, 256), f32),
            pltpu.VMEM((steps, rows, 256), f32),
            pltpu.VMEM((chips, ns, rows, 256), bf16),
            pltpu.VMEM((chips, ns, rows, 256), bf16),
            pltpu.VMEM((ns, rows, 256), f32),
            pltpu.VMEM((ns, rows, 256), bf16),
            pltpu.VMEM((ns, rows, 256), bf16),
            pltpu.VMEM((2, 2 * SW + HALO, FR), bf16),
            pltpu.VMEM((nf, high, 256), bf16),
            pltpu.VMEM((nf, high, 256), bf16),
            pltpu.VMEM((blocks, SW, 256), bf16),
            pltpu.VMEM((SCD, 2 * high, SW), bf16),
            sems((7,)),
            sems((steps,)), sems((steps,)),
            sems((chips, ns)), sems((chips, ns)),
            sems((ns,)), sems((ns,)),
            sems((nf,)), sems((nf,)),
        ],
        compiler_params=pltpu.CompilerParams(
            collective_id=0, has_side_effects=True, vmem_limit_bytes=56 * 1024 * 1024
        ),
    )(
        column_offsets, row_offsets, block_column[0, 0], facet_model[0],
        cell_rows[0], cell_columns[0], cell_fraction[0, 0],
    )
    return result[None, None]


def solution(mesh):
    in_specs = (
        P("facet", "sub", None),
        P(),
        P(),
        P("facet", "sub", None),
        P("facet", "sub", None),
        P("facet", "sub", None),
        P("facet", "sub", None, None),
    )
    out_specs = P("facet", "sub", None, None)
    return jax.shard_map(
        per_device, mesh=mesh, in_specs=in_specs, out_specs=out_specs, check_vma=False
    )
```

```python
import functools
import math

import jax
import jax.numpy as jnp
from jax import lax
from jax.experimental import pallas as pl
from jax.experimental.pallas import tpu as pltpu
from jax.sharding import PartitionSpec as P

MESH = pl.DeviceIdType.MESH
FX = 8192
GRID = 65536
FR = 512
SW = 512
SCD = 2
ROW_FACETS = 8
HALO = 16
CHUNK = 128
DEPTH = 1024
HALF = DEPTH // 2
GROUP = 32
SETTLE = 2
PASS_AT = 1
PASS_LAG = 2
SPREAD = 0.98


def cos_sin(turns, whole=GRID):
    shift = (whole // 4).bit_length() - 1
    quadrant = (turns + whole // 8) >> shift
    rest = turns - (quadrant << shift)
    theta = rest.astype(jnp.float32) * (2.0 * math.pi / whole)
    t2 = theta * theta
    sine = theta * (1.0 + t2 * (-1.0 / 6 + t2 * (1.0 / 120 + t2 * (-1.0 / 5040 + t2 * (1.0 / 362880)))))
    cosine = 1.0 + t2 * (-0.5 + t2 * (1.0 / 24 + t2 * (-1.0 / 720 + t2 * (1.0 / 40320 - t2 * (1.0 / 3628800)))))
    odd = (quadrant & 1) == 1
    c = jnp.where(odd, sine, cosine)
    s = jnp.where(odd, cosine, sine)
    c = jnp.where(((quadrant + 1) & 2) == 2, -c, c)
    s = jnp.where((quadrant & 2) == 2, -s, s)
    return c, s


def predict_kernel(
    nf, ns, rows, strip, scale,
    columns_hbm, rows_hbm, block_hbm, x_hbm, cell_v_hbm, cell_u_hbm, fraction_hbm, out_ref,
    columns_ref, rows_ref, block_ref, cell_v_ref, cell_u_ref, fraction_ref, x_ref, even_ref, odd_ref, table0, table1, turn0, turn1, pairs, sib_send, sib_recv,
    send1, recv1, own, send2, recv2, vy, send3, recv3, weights, planes,
    in_sems, x_sems, ssem0, rsem0, ssem1, rsem1, ssem2, rsem2, ssem3, rsem3,
):
    bf16, f32 = jnp.bfloat16, jnp.float32
    facet = lax.axis_index("facet")
    sub = lax.axis_index("sub")
    frow = facet // ROW_FACETS
    fcol = facet % ROW_FACETS
    base = frow * ROW_FACETS
    chip = fcol // 2
    core = fcol % 2
    parts = FX // DEPTH
    chips = ROW_FACETS // 2
    steps = chips * ns
    high = strip + HALO

    loads = [
        pltpu.make_async_copy(source, target, in_sems.at[n])
        for n, (source, target) in enumerate([
            (columns_hbm, columns_ref), (rows_hbm, rows_ref), (block_hbm, block_ref),
            (cell_v_hbm, cell_v_ref), (cell_u_hbm, cell_u_ref), (fraction_hbm, fraction_ref),
        ])
    ]
    x_loads = [
        pltpu.make_async_copy(
            x_hbm.at[:, a * DEPTH:(a + 1) * DEPTH], x_ref.at[:, a * DEPTH:(a + 1) * DEPTH], x_sems.at[a])
        for a in range(parts)
    ]
    for load in loads[:1] + x_loads + loads[1:]:
        load.start()
    barrier = pltpu.get_barrier_semaphore()
    for k in range(1, nf):
        pl.semaphore_signal(barrier, inc=1, device_id={"facet": (facet + k) % nf}, device_id_type=MESH)
    for k in range(1, ns):
        pl.semaphore_signal(barrier, inc=1, device_id={"sub": (sub + k) % ns}, device_id_type=MESH)

    def place(t):
        far = chips - 1 - t % chips
        other = (chip // 2 + far // 2) % 2 * 2 + (chip % 2 + far % 2) % 2
        return other, (sub + 1 + t // chips) % ns

    x_first = fcol * FX

    def step_turns(t, turn):
        q, group = place(t)
        lane = lax.broadcasted_iota(jnp.int32, (64, 256), 1)
        line = lax.broadcasted_iota(jnp.int32, (64, 256), 0)
        u = columns_ref[group * SCD + q // 2] + 8 * (q % 2 * 256 + lane)
        x = jnp.where(line < 32, 32 * line, jnp.where(line < 48, 2 * (line - 32) + 1, 2 * (x_first + DEPTH * (line - 48)) + DEPTH - 1))
        c, s = cos_sin((x * u) & (2 * GRID - 1), 2 * GRID)
        turn[0] = c
        turn[1] = s

    def table_rows(turn, table, first, last):
        fc, fs = turn[0, 32:48], turn[1, 32:48]
        for g in range(first, last):
            c0, s0 = turn[0, g:g + 1], turn[1, g:g + 1]
            table[g * 16:(g + 1) * 16, 0:256] = (c0 * fc - s0 * fs).astype(bf16)
            table[g * 16:(g + 1) * 16, 256:512] = (s0 * fc + c0 * fs).astype(bf16)

    def fold():
        line = lax.broadcasted_iota(jnp.int32, (256, 256), 0)
        lane = lax.broadcasted_iota(jnp.int32, (256, 256), 1)
        flip = jnp.where(line + lane == 255, 1.0, 0.0).astype(bf16)
        for a in range(parts):
            x_loads[a].wait()
            for k in range(HALF // 256):
                low = x_ref[:, a * DEPTH + HALF - (k + 1) * 256:a * DEPTH + HALF - k * 256]
                low = jnp.dot(low, flip, preferred_element_type=f32)
                high_half = x_ref[:, a * DEPTH + HALF + k * 256:a * DEPTH + HALF + (k + 1) * 256].astype(f32)
                even = (high_half + low).astype(bf16)
                odd = (high_half - low).astype(bf16)
                for r in range(rows // 16):
                    at = (r * parts + a) * 16
                    even_ref[at:at + 16, k * 256:(k + 1) * 256] = even[r * 16:(r + 1) * 16]
                    odd_ref[at:at + 16, k * 256:(k + 1) * 256] = odd[r * 16:(r + 1) * 16]

    def build_vy():
        y = frow * FX + lax.broadcasted_iota(jnp.int32, (16, FR), 1)
        low = lax.broadcasted_iota(jnp.int32, (16, FR), 0)
        fine_c, fine_s = cos_sin((128 * low * y) & (GRID - 1))
        for r in range(2):
            yh = frow * FX + lax.broadcasted_iota(jnp.int32, (32, FR), 1)
            upper = rows_ref[r] + 2048 * lax.broadcasted_iota(jnp.int32, (32, FR), 0)
            cc, cs = cos_sin((upper * yh) & (GRID - 1))
            for g in range(32):
                at = r * SW + g * 16
                c0, s0 = cc[g:g + 1], cs[g:g + 1]
                vy[0, at:at + 16, :] = (c0 * fine_c - s0 * fine_s).astype(bf16)
                vy[1, at:at + 16, :] = (s0 * fine_c + c0 * fine_s).astype(bf16)
        vy[:, 2 * SW:, :] = jnp.zeros((2, HALO, FR), bf16)

    def copy0(t):
        return pltpu.make_async_remote_copy(
            src_ref=sib_send.at[t], dst_ref=sib_recv.at[t],
            send_sem=ssem0.at[t], recv_sem=rsem0.at[t],
            device_id={"facet": base + 2 * chip + 1 - core}, device_id_type=MESH,
        )

    def copy1(target, group, source):
        return pltpu.make_async_remote_copy(
            src_ref=send1.at[target, group], dst_ref=recv1.at[source, group],
            send_sem=ssem1.at[target, group], recv_sem=rsem1.at[source, group],
            device_id={"facet": base + 2 * target + core}, device_id_type=MESH,
        )

    def copy2(target, source):
        return pltpu.make_async_remote_copy(
            src_ref=send2.at[target], dst_ref=recv2.at[source],
            send_sem=ssem2.at[target], recv_sem=rsem2.at[source],
            device_id={"sub": target}, device_id_type=MESH,
        )

    def copy3(target, source):
        return pltpu.make_async_remote_copy(
            src_ref=send3.at[target], dst_ref=recv3.at[source],
            send_sem=ssem3.at[target], recv_sem=rsem3.at[source],
            device_id={"facet": target}, device_id_type=MESH,
        )

    def compute(t, table, turn, pair, next_table, next_turn, first=False):
        step_turns((t + 1) % steps, next_turn)
        group_rows = min(rows, GROUP)
        count = rows // group_rows
        for r in range(count):
            at = r * group_rows
            lines = pl.ds(at * parts, group_rows * parts)
            zc_all = jnp.dot(even_ref[lines, :], table[:, 0:256], preferred_element_type=f32)
            zs_all = jnp.dot(odd_ref[lines, :], table[:, 256:512], preferred_element_type=f32)
            for h in range(0, group_rows, 16):
                real = jnp.zeros((16, 256), f32)
                imag = jnp.zeros((16, 256), f32)
                for a in range(parts):
                    zc = zc_all[h * parts + a * 16:h * parts + (a + 1) * 16]
                    zs = zs_all[h * parts + a * 16:h * parts + (a + 1) * 16]
                    wc, ws = turn[0, 48 + a:49 + a], turn[1, 48 + a:49 + a]
                    real = real + (wc * zc - ws * zs)
                    imag = imag - (ws * zc + wc * zs)
                for k in range(2):
                    pair[k, at + h:at + h + 16, 0:128] = real[:, k * 128:(k + 1) * 128]
                    pair[k, at + h:at + h + 16, 128:256] = imag[:, k * 128:(k + 1) * 128]
            table_rows(next_turn, next_table, r * 32 // count, (r + 1) * 32 // count)
        sib_send[t] = pair[1 - core]
        if first:
            pl.semaphore_wait(barrier, nf - 1 + ns - 1)
        copy0(t).start()

    def combine(t, pair, last):
        q, group = place(t)
        copy0(t).wait_recv()
        both = pair[core] + sib_recv[t]
        if last:
            own[group] = both
        else:
            send1[q, group] = both.astype(bf16)
            copy1(q, group, chip).start()

    def gather(group):
        for j in range(1, chips):
            copy1(chip, group, (chip + j) % chips).wait_recv()
        total = own[group]
        for j in range(1, chips):
            total = total + recv1[(chip + j) % chips, group].astype(f32)
        return total.astype(bf16)

    loads[0].wait()
    step_turns(0, turn0)
    table_rows(turn0, table0, 0, 32)
    fold()

    tables = (table0, table1)
    turns = (turn0, turn1)

    def settle(t, at):
        combine(t, pairs.at[at % 4], at % chips == chips - 1)

    def pass_on(g):
        group = (sub + 1 + g) % ns
        send2[group] = gather(group)
        copy2(group, sub).start()

    def four_steps(g, first=0):
        t = chips * g
        for j in range(chips):
            compute(t + j, tables[j % 2], turns[j % 2], pairs.at[j], tables[1 - j % 2], turns[1 - j % 2], first == 0 and j == 0)
            if first > 0 or j >= SETTLE:
                settle(t + j - SETTLE, j - SETTLE)
            if j == PASS_AT and first >= PASS_LAG:
                pass_on(g - PASS_LAG)

    def more_steps(g, carry):
        four_steps(g, PASS_LAG)
        return carry

    for g in range(PASS_LAG):
        four_steps(g, g)
    lax.fori_loop(PASS_LAG, ns, more_steps, 0)
    for j in range(SETTLE):
        settle(steps - SETTLE + j, chips - SETTLE + j)
    for g in range(ns - PASS_LAG, ns - 1):
        pass_on(g)
    loads[1].wait()
    build_vy()
    recv2[sub] = gather(sub)
    for k in range(1, ns):
        copy2(sub, (sub + k) % ns).wait_recv()

    partial = recv2[...].reshape(ns * rows, 2 * CHUNK)

    for k in range(1, nf + 1):
        target = (facet + k) % nf
        at = pl.ds(pl.multiple_of(target * strip, 16), high)
        first = jnp.dot(vy[0, at, :], partial, preferred_element_type=f32)
        second = jnp.dot(vy[1, at, :], partial, preferred_element_type=f32)
        send3[target, :, 0:128] = (first[:, 0:128] + second[:, 128:256]).astype(bf16)
        send3[target, :, 128:256] = (first[:, 128:256] - second[:, 0:128]).astype(bf16)
        if k < nf:
            copy3(target, facet).start()

    recv3[facet] = send3[facet]

    for load in loads[2:]:
        load.wait()
    blocks = cell_v_ref.shape[1] // 128
    root = math.sqrt(math.log2(math.e) / SPREAD)

    def taps(cell, fraction, extent):
        position = lax.broadcasted_iota(jnp.int32, (extent, 128), 0)
        offset = position.astype(f32) * root - (cell.astype(f32) + 1.0 + fraction) * root
        distance = position - cell
        return jnp.where((distance & -4) == 0, jnp.exp2(-(offset * offset)), 0.0)

    def build_weights(b, carry):
        at = pl.ds(pl.multiple_of(b * 128, 128), 128)
        w = taps(cell_u_ref[:, at], fraction_ref[1:2, at], SW)
        upper = w.astype(bf16)
        weights[b, :, 0:128] = upper
        weights[b, :, 128:256] = (w - upper.astype(f32)).astype(bf16)
        return carry

    lax.fori_loop(0, blocks, build_weights, 0, unroll=2)

    def drain0(t, carry):
        copy0(t).wait_send()
        return carry

    def drain1(n, carry):
        copy1((chip + 1 + n // ns) % chips, n % ns, chip).wait_send()
        return carry

    lax.fori_loop(0, steps, drain0, 0)
    lax.fori_loop(0, (chips - 1) * ns, drain1, 0)
    for k in range(1, ns):
        copy2((sub + k) % ns, sub).wait_send()
    for k in range(1, nf):
        copy3(facet, (facet + k) % nf).wait_recv()
    for column in range(SCD):
        for j in range(SW // CHUNK):
            chunk = column * (SW // CHUNK) + j
            total = recv3[chunk]
            if nf > ROW_FACETS:
                total = total.astype(f32)
                for other in range(1, nf // ROW_FACETS):
                    total = total + recv3[other * ROW_FACETS + chunk].astype(f32)
                total = total.astype(bf16)
            planes[column, 0:high, j * 128:(j + 1) * 128] = total[:, 0:128]
            planes[column, high:2 * high, j * 128:(j + 1) * 128] = total[:, 128:256]

    def degrid(b, carry):
        at = pl.ds(pl.multiple_of(b * 128, 128), 128)
        mixed = jnp.dot(planes[block_ref[b]], weights[b], preferred_element_type=f32)
        mixed = mixed[:, 0:128] + mixed[:, 128:256]
        row_weight = taps(cell_v_ref[:, at], fraction_ref[0:1, at], high) * scale
        out_ref[0:1, at] = jnp.sum(mixed[:high] * row_weight, axis=0, keepdims=True)
        out_ref[1:2, at] = jnp.sum(mixed[high:] * row_weight, axis=0, keepdims=True)
        return carry

    lax.fori_loop(0, blocks, degrid, 0, unroll=16)

    for k in range(1, nf):
        copy3((facet + k) % nf, facet).wait_send()


def per_device(
    facet_model, column_offsets, row_offsets, block_column, cell_rows, cell_columns, cell_fraction
):
    nf = lax.axis_size("facet")
    ns = lax.axis_size("sub")
    rows = facet_model.shape[1]
    strip = 2 * SW // nf
    high = strip + HALO
    total = cell_rows.shape[-1]
    blocks = total // 128
    chips = ROW_FACETS // 2
    steps = chips * ns
    vmem = pl.BlockSpec(memory_space=pltpu.VMEM)
    bf16, f32 = jnp.bfloat16, jnp.float32
    sems = pltpu.SemaphoreType.DMA
    result = pl.pallas_call(
        functools.partial(predict_kernel, nf, ns, rows, strip, 1.0 / math.sqrt(nf * FR * FX)),
        out_shape=jax.ShapeDtypeStruct((2, total), f32),
        in_specs=[pl.BlockSpec(memory_space=pltpu.HBM)] * 7,
        out_specs=vmem,
        scratch_shapes=[
            pltpu.SMEM(column_offsets.shape, jnp.int32),
            pltpu.SMEM(row_offsets.shape, jnp.int32),
            pltpu.SMEM((blocks,), jnp.int32),
            pltpu.VMEM((1, total), jnp.int32),
            pltpu.VMEM((1, total), jnp.int32),
            pltpu.VMEM((2, total), f32),
            pltpu.VMEM((rows, FX), bf16),
            pltpu.VMEM((rows * FX // DEPTH, HALF), bf16),
            pltpu.VMEM((rows * FX // DEPTH, HALF), bf16),
            pltpu.VMEM((HALF, 512), bf16),
            pltpu.VMEM((HALF, 512), bf16),
            pltpu.VMEM((2, 64, 256), f32),
            pltpu.VMEM((2, 64, 256), f32),
            pltpu.VMEM((4, 2, rows, 256), f32),
            pltpu.VMEM((steps, rows, 256), f32),
            pltpu.VMEM((steps, rows, 256), f32),
            pltpu.VMEM((chips, ns, rows, 256), bf16),
            pltpu.VMEM((chips, ns, rows, 256), bf16),
            pltpu.VMEM((ns, rows, 256), f32),
            pltpu.VMEM((ns, rows, 256), bf16),
            pltpu.VMEM((ns, rows, 256), bf16),
            pltpu.VMEM((2, 2 * SW + HALO, FR), bf16),
            pltpu.VMEM((nf, high, 256), bf16),
            pltpu.VMEM((nf, high, 256), bf16),
            pltpu.VMEM((blocks, SW, 256), bf16),
            pltpu.VMEM((SCD, 2 * high, SW), bf16),
            sems((6,)),
            sems((FX // DEPTH,)),
            sems((steps,)), sems((steps,)),
            sems((chips, ns)), sems((chips, ns)),
            sems((ns,)), sems((ns,)),
            sems((nf,)), sems((nf,)),
        ],
        compiler_params=pltpu.CompilerParams(
            collective_id=0, has_side_effects=True, vmem_limit_bytes=56 * 1024 * 1024
        ),
    )(
        column_offsets, row_offsets, block_column[0, 0], facet_model[0],
        cell_rows[0], cell_columns[0], cell_fraction[0, 0],
    )
    return result[None, None]


def solution(mesh):
    in_specs = (
        P("facet", "sub", None),
        P(),
        P(),
        P("facet", "sub", None),
        P("facet", "sub", None),
        P("facet", "sub", None),
        P("facet", "sub", None, None),
    )
    out_specs = P("facet", "sub", None, None)
    return jax.shard_map(
        per_device, mesh=mesh, in_specs=in_specs, out_specs=out_specs, check_vma=False
    )
```

```python
import functools
import math

import jax
import jax.numpy as jnp
from jax import lax
from jax.experimental import pallas as pl
from jax.experimental.pallas import tpu as pltpu
from jax.sharding import PartitionSpec as P

MESH = pl.DeviceIdType.MESH
FX = 8192
GRID = 65536
FR = 512
SW = 512
SCD = 2
ROW_FACETS = 8
HALO = 16
CHUNK = 128
DEPTH = 1024
HALF = DEPTH // 2
GROUP = 32
SETTLE = 2
PASS_AT = 1
PASS_LAG = 2
SPREAD = 0.98


def cos_sin(turns, whole=GRID):
    shift = (whole // 4).bit_length() - 1
    quadrant = (turns + whole // 8) >> shift
    rest = turns - (quadrant << shift)
    theta = rest.astype(jnp.float32) * (2.0 * math.pi / whole)
    t2 = theta * theta
    sine = theta * (1.0 + t2 * (-1.0 / 6 + t2 * (1.0 / 120 + t2 * (-1.0 / 5040 + t2 * (1.0 / 362880)))))
    cosine = 1.0 + t2 * (-0.5 + t2 * (1.0 / 24 + t2 * (-1.0 / 720 + t2 * (1.0 / 40320 - t2 * (1.0 / 3628800)))))
    odd = (quadrant & 1) == 1
    c = jnp.where(odd, sine, cosine)
    s = jnp.where(odd, cosine, sine)
    c = jnp.where(((quadrant + 1) & 2) == 2, -c, c)
    s = jnp.where((quadrant & 2) == 2, -s, s)
    return c, s


def predict_kernel(
    nf, ns, rows, strip, scale,
    columns_hbm, rows_hbm, block_hbm, x_hbm, cell_v_hbm, cell_u_hbm, fraction_hbm, out_ref,
    columns_ref, rows_ref, block_ref, cell_v_ref, cell_u_ref, fraction_ref, x_ref, even_ref, odd_ref, table0, table1, turn0, turn1, pairs, sib_send, sib_recv,
    send1, recv1, own, send2, recv2, vy, send3, recv3, weights, planes,
    in_sems, x_sems, ssem0, rsem0, ssem1, rsem1, ssem2, rsem2, ssem3, rsem3,
):
    bf16, f32 = jnp.bfloat16, jnp.float32
    facet = lax.axis_index("facet")
    sub = lax.axis_index("sub")
    frow = facet // ROW_FACETS
    fcol = facet % ROW_FACETS
    base = frow * ROW_FACETS
    chip = fcol // 2
    core = fcol % 2
    parts = FX // DEPTH
    chips = ROW_FACETS // 2
    steps = chips * ns
    high = strip + HALO

    loads = [
        pltpu.make_async_copy(source, target, in_sems.at[n])
        for n, (source, target) in enumerate([
            (columns_hbm, columns_ref), (rows_hbm, rows_ref), (block_hbm, block_ref),
            (cell_v_hbm, cell_v_ref), (cell_u_hbm, cell_u_ref), (fraction_hbm, fraction_ref),
        ])
    ]
    x_loads = [
        pltpu.make_async_copy(
            x_hbm.at[:, a * DEPTH:(a + 1) * DEPTH], x_ref.at[:, a * DEPTH:(a + 1) * DEPTH], x_sems.at[a])
        for a in range(parts)
    ]
    for load in loads[:1] + x_loads + loads[1:]:
        load.start()
    barrier = pltpu.get_barrier_semaphore()
    for k in range(1, nf):
        pl.semaphore_signal(barrier, inc=1, device_id={"facet": (facet + k) % nf}, device_id_type=MESH)
    for k in range(1, ns):
        pl.semaphore_signal(barrier, inc=1, device_id={"sub": (sub + k) % ns}, device_id_type=MESH)

    def place(t):
        far = chips - 1 - t % chips
        other = (chip // 2 + far // 2) % 2 * 2 + (chip % 2 + far % 2) % 2
        return other, (sub + 1 + t // chips) % ns

    x_first = fcol * FX

    def step_turns(t, turn):
        q, group = place(t)
        lane = lax.broadcasted_iota(jnp.int32, (64, 256), 1)
        line = lax.broadcasted_iota(jnp.int32, (64, 256), 0)
        u = columns_ref[group * SCD + q // 2] + 8 * (q % 2 * 256 + lane)
        x = jnp.where(line < 32, 32 * line, jnp.where(line < 48, 2 * (line - 32) + 1, 2 * (x_first + DEPTH * (line - 48)) + DEPTH - 1))
        c, s = cos_sin((x * u) & (2 * GRID - 1), 2 * GRID)
        turn[0] = c
        turn[1] = s

    def table_rows(turn, table, first, last):
        fc, fs = turn[0, 32:48], turn[1, 32:48]
        for g in range(first, last):
            c0, s0 = turn[0, g:g + 1], turn[1, g:g + 1]
            table[g * 16:(g + 1) * 16, 0:256] = (c0 * fc - s0 * fs).astype(bf16)
            table[g * 16:(g + 1) * 16, 256:512] = (s0 * fc + c0 * fs).astype(bf16)

    def fold():
        line = lax.broadcasted_iota(jnp.int32, (256, 256), 0)
        lane = lax.broadcasted_iota(jnp.int32, (256, 256), 1)
        flip = jnp.where(line + lane == 255, 1.0, 0.0).astype(bf16)
        for a in range(parts):
            x_loads[a].wait()
            for k in range(HALF // 256):
                low = x_ref[:, a * DEPTH + HALF - (k + 1) * 256:a * DEPTH + HALF - k * 256]
                low = jnp.dot(low, flip, preferred_element_type=f32)
                high_half = x_ref[:, a * DEPTH + HALF + k * 256:a * DEPTH + HALF + (k + 1) * 256].astype(f32)
                even = (high_half + low).astype(bf16)
                odd = (high_half - low).astype(bf16)
                for r in range(rows // 16):
                    at = (r * parts + a) * 16
                    even_ref[at:at + 16, k * 256:(k + 1) * 256] = even[r * 16:(r + 1) * 16]
                    odd_ref[at:at + 16, k * 256:(k + 1) * 256] = odd[r * 16:(r + 1) * 16]

    def build_vy():
        y = frow * FX + lax.broadcasted_iota(jnp.int32, (16, FR), 1)
        low = lax.broadcasted_iota(jnp.int32, (16, FR), 0)
        fine_c, fine_s = cos_sin((128 * low * y) & (GRID - 1))
        for r in range(2):
            yh = frow * FX + lax.broadcasted_iota(jnp.int32, (32, FR), 1)
            upper = rows_ref[r] + 2048 * lax.broadcasted_iota(jnp.int32, (32, FR), 0)
            cc, cs = cos_sin((upper * yh) & (GRID - 1))
            for g in range(32):
                at = r * SW + g * 16
                c0, s0 = cc[g:g + 1], cs[g:g + 1]
                vy[0, at:at + 16, :] = (c0 * fine_c - s0 * fine_s).astype(bf16)
                vy[1, at:at + 16, :] = (s0 * fine_c + c0 * fine_s).astype(bf16)
        vy[:, 2 * SW:, :] = jnp.zeros((2, HALO, FR), bf16)

    def copy0(t):
        return pltpu.make_async_remote_copy(
            src_ref=sib_send.at[t], dst_ref=sib_recv.at[t],
            send_sem=ssem0.at[t], recv_sem=rsem0.at[t],
            device_id={"facet": base + 2 * chip + 1 - core}, device_id_type=MESH,
        )

    def copy1(target, group, source):
        return pltpu.make_async_remote_copy(
            src_ref=send1.at[target, group], dst_ref=recv1.at[source, group],
            send_sem=ssem1.at[target, group], recv_sem=rsem1.at[source, group],
            device_id={"facet": base + 2 * target + core}, device_id_type=MESH,
        )

    def copy2(target, source):
        return pltpu.make_async_remote_copy(
            src_ref=send2.at[target], dst_ref=recv2.at[source],
            send_sem=ssem2.at[target], recv_sem=rsem2.at[source],
            device_id={"sub": target}, device_id_type=MESH,
        )

    def copy3(target, source):
        return pltpu.make_async_remote_copy(
            src_ref=send3.at[target], dst_ref=recv3.at[source],
            send_sem=ssem3.at[target], recv_sem=rsem3.at[source],
            device_id={"facet": target}, device_id_type=MESH,
        )

    def compute(t, table, turn, pair, next_table, next_turn, first=False):
        step_turns((t + 1) % steps, next_turn)
        group_rows = min(rows, GROUP)
        count = rows // group_rows
        for r in range(count):
            at = r * group_rows
            lines = pl.ds(at * parts, group_rows * parts)
            zc_all = jnp.dot(even_ref[lines, :], table[:, 0:256], preferred_element_type=f32)
            zs_all = jnp.dot(odd_ref[lines, :], table[:, 256:512], preferred_element_type=f32)
            for h in range(0, group_rows, 16):
                real = jnp.zeros((16, 256), f32)
                imag = jnp.zeros((16, 256), f32)
                for a in range(parts):
                    zc = zc_all[h * parts + a * 16:h * parts + (a + 1) * 16]
                    zs = zs_all[h * parts + a * 16:h * parts + (a + 1) * 16]
                    wc, ws = turn[0, 48 + a:49 + a], turn[1, 48 + a:49 + a]
                    real = real + (wc * zc - ws * zs)
                    imag = imag - (ws * zc + wc * zs)
                for k in range(2):
                    pair[k, at + h:at + h + 16, 0:128] = real[:, k * 128:(k + 1) * 128]
                    pair[k, at + h:at + h + 16, 128:256] = imag[:, k * 128:(k + 1) * 128]
            table_rows(next_turn, next_table, r * 32 // count, (r + 1) * 32 // count)
        sib_send[t] = pair[1 - core]
        if first == 1:
            return
        if first == 2:
            pl.semaphore_wait(barrier, nf - 1 + ns - 1)
            copy0(t - 1).start()
        copy0(t).start()

    def combine(t, pair, last):
        q, group = place(t)
        copy0(t).wait_recv()
        both = pair[core] + sib_recv[t]
        if last:
            own[group] = both
        else:
            send1[q, group] = both.astype(bf16)
            copy1(q, group, chip).start()

    def gather(group):
        for j in range(1, chips):
            copy1(chip, group, (chip + j) % chips).wait_recv()
        total = own[group]
        for j in range(1, chips):
            total = total + recv1[(chip + j) % chips, group].astype(f32)
        return total.astype(bf16)

    loads[0].wait()
    step_turns(0, turn0)
    table_rows(turn0, table0, 0, 32)
    fold()

    tables = (table0, table1)
    turns = (turn0, turn1)

    def settle(t, at):
        combine(t, pairs.at[at % 4], at % chips == chips - 1)

    def pass_on(g):
        group = (sub + 1 + g) % ns
        send2[group] = gather(group)
        copy2(group, sub).start()

    def four_steps(g, first=0):
        t = chips * g
        for j in range(chips):
            compute(t + j, tables[j % 2], turns[j % 2], pairs.at[j], tables[1 - j % 2], turns[1 - j % 2], j + 1 if first == 0 and j < 2 else 0)
            if first > 0 or j >= SETTLE:
                settle(t + j - SETTLE, j - SETTLE)
            if j == PASS_AT and first >= PASS_LAG:
                pass_on(g - PASS_LAG)

    def more_steps(g, carry):
        four_steps(g, PASS_LAG)
        return carry

    for g in range(PASS_LAG):
        four_steps(g, g)
    lax.fori_loop(PASS_LAG, ns, more_steps, 0)
    for j in range(SETTLE):
        settle(steps - SETTLE + j, chips - SETTLE + j)
    for g in range(ns - PASS_LAG, ns - 1):
        pass_on(g)
    loads[1].wait()
    build_vy()
    recv2[sub] = gather(sub)
    for k in range(1, ns):
        copy2(sub, (sub + k) % ns).wait_recv()

    partial = recv2[...].reshape(ns * rows, 2 * CHUNK)

    for k in range(1, nf + 1):
        target = (facet + k) % nf
        at = pl.ds(pl.multiple_of(target * strip, 16), high)
        first = jnp.dot(vy[0, at, :], partial, preferred_element_type=f32)
        second = jnp.dot(vy[1, at, :], partial, preferred_element_type=f32)
        send3[target, :, 0:128] = (first[:, 0:128] + second[:, 128:256]).astype(bf16)
        send3[target, :, 128:256] = (first[:, 128:256] - second[:, 0:128]).astype(bf16)
        if k < nf:
            copy3(target, facet).start()

    recv3[facet] = send3[facet]

    for load in loads[2:]:
        load.wait()
    blocks = cell_v_ref.shape[1] // 128
    root = math.sqrt(math.log2(math.e) / SPREAD)

    def taps(cell, fraction, extent):
        position = lax.broadcasted_iota(jnp.int32, (extent, 128), 0)
        offset = position.astype(f32) * root - (cell.astype(f32) + 1.0 + fraction) * root
        distance = position - cell
        return jnp.where((distance & -4) == 0, jnp.exp2(-(offset * offset)), 0.0)

    def build_weights(b, carry):
        at = pl.ds(pl.multiple_of(b * 128, 128), 128)
        w = taps(cell_u_ref[:, at], fraction_ref[1:2, at], SW)
        upper = w.astype(bf16)
        weights[b, :, 0:128] = upper
        weights[b, :, 128:256] = (w - upper.astype(f32)).astype(bf16)
        return carry

    lax.fori_loop(0, blocks, build_weights, 0, unroll=2)

    def drain0(t, carry):
        copy0(t).wait_send()
        return carry

    def drain1(n, carry):
        copy1((chip + 1 + n // ns) % chips, n % ns, chip).wait_send()
        return carry

    lax.fori_loop(0, steps, drain0, 0)
    lax.fori_loop(0, (chips - 1) * ns, drain1, 0)
    for k in range(1, ns):
        copy2((sub + k) % ns, sub).wait_send()
    for k in range(1, nf):
        copy3(facet, (facet + k) % nf).wait_recv()
    for column in range(SCD):
        for j in range(SW // CHUNK):
            chunk = column * (SW // CHUNK) + j
            total = recv3[chunk]
            if nf > ROW_FACETS:
                total = total.astype(f32)
                for other in range(1, nf // ROW_FACETS):
                    total = total + recv3[other * ROW_FACETS + chunk].astype(f32)
                total = total.astype(bf16)
            planes[column, 0:high, j * 128:(j + 1) * 128] = total[:, 0:128]
            planes[column, high:2 * high, j * 128:(j + 1) * 128] = total[:, 128:256]

    def degrid(b, carry):
        at = pl.ds(pl.multiple_of(b * 128, 128), 128)
        mixed = jnp.dot(planes[block_ref[b]], weights[b], preferred_element_type=f32)
        mixed = mixed[:, 0:128] + mixed[:, 128:256]
        row_weight = taps(cell_v_ref[:, at], fraction_ref[0:1, at], high) * scale
        out_ref[0:1, at] = jnp.sum(mixed[:high] * row_weight, axis=0, keepdims=True)
        out_ref[1:2, at] = jnp.sum(mixed[high:] * row_weight, axis=0, keepdims=True)
        return carry

    lax.fori_loop(0, blocks, degrid, 0, unroll=32)

    for k in range(1, nf):
        copy3((facet + k) % nf, facet).wait_send()


def per_device(
    facet_model, column_offsets, row_offsets, block_column, cell_rows, cell_columns, cell_fraction
):
    nf = lax.axis_size("facet")
    ns = lax.axis_size("sub")
    rows = facet_model.shape[1]
    strip = 2 * SW // nf
    high = strip + HALO
    total = cell_rows.shape[-1]
    blocks = total // 128
    chips = ROW_FACETS // 2
    steps = chips * ns
    vmem = pl.BlockSpec(memory_space=pltpu.VMEM)
    bf16, f32 = jnp.bfloat16, jnp.float32
    sems = pltpu.SemaphoreType.DMA
    result = pl.pallas_call(
        functools.partial(predict_kernel, nf, ns, rows, strip, 1.0 / math.sqrt(nf * FR * FX)),
        out_shape=jax.ShapeDtypeStruct((2, total), f32),
        in_specs=[pl.BlockSpec(memory_space=pltpu.HBM)] * 7,
        out_specs=vmem,
        scratch_shapes=[
            pltpu.SMEM(column_offsets.shape, jnp.int32),
            pltpu.SMEM(row_offsets.shape, jnp.int32),
            pltpu.SMEM((blocks,), jnp.int32),
            pltpu.VMEM((1, total), jnp.int32),
            pltpu.VMEM((1, total), jnp.int32),
            pltpu.VMEM((2, total), f32),
            pltpu.VMEM((rows, FX), bf16),
            pltpu.VMEM((rows * FX // DEPTH, HALF), bf16),
            pltpu.VMEM((rows * FX // DEPTH, HALF), bf16),
            pltpu.VMEM((HALF, 512), bf16),
            pltpu.VMEM((HALF, 512), bf16),
            pltpu.VMEM((2, 64, 256), f32),
            pltpu.VMEM((2, 64, 256), f32),
            pltpu.VMEM((4, 2, rows, 256), f32),
            pltpu.VMEM((steps, rows, 256), f32),
            pltpu.VMEM((steps, rows, 256), f32),
            pltpu.VMEM((chips, ns, rows, 256), bf16),
            pltpu.VMEM((chips, ns, rows, 256), bf16),
            pltpu.VMEM((ns, rows, 256), f32),
            pltpu.VMEM((ns, rows, 256), bf16),
            pltpu.VMEM((ns, rows, 256), bf16),
            pltpu.VMEM((2, 2 * SW + HALO, FR), bf16),
            pltpu.VMEM((nf, high, 256), bf16),
            pltpu.VMEM((nf, high, 256), bf16),
            pltpu.VMEM((blocks, SW, 256), bf16),
            pltpu.VMEM((SCD, 2 * high, SW), bf16),
            sems((6,)),
            sems((FX // DEPTH,)),
            sems((steps,)), sems((steps,)),
            sems((chips, ns)), sems((chips, ns)),
            sems((ns,)), sems((ns,)),
            sems((nf,)), sems((nf,)),
        ],
        compiler_params=pltpu.CompilerParams(
            collective_id=0, has_side_effects=True, vmem_limit_bytes=56 * 1024 * 1024
        ),
    )(
        column_offsets, row_offsets, block_column[0, 0], facet_model[0],
        cell_rows[0], cell_columns[0], cell_fraction[0, 0],
    )
    return result[None, None]


def solution(mesh):
    in_specs = (
        P("facet", "sub", None),
        P(),
        P(),
        P("facet", "sub", None),
        P("facet", "sub", None),
        P("facet", "sub", None),
        P("facet", "sub", None, None),
    )
    out_specs = P("facet", "sub", None, None)
    return jax.shard_map(
        per_device, mesh=mesh, in_specs=in_specs, out_specs=out_specs, check_vma=False
    )
```
